32 devices in a mesh: ctx: 8 (over y, x, core), head: 4 (over z).
Axes of the slice: x: 2, y: 2, z: 4, core: 2. Of those that a mesh axis runs over, the one named last changes fastest.
Arguments:
- block_order: int32 [16], replicated, may hold values from 0 to 15, as said below
- query_latent: bfloat16 [1024, 128, 576], P('ctx', 'head'), may hold values from -12 to 12
- key_latent: bfloat16 [1024, 576], P('ctx'), may hold values from -6 to 6
- normalizer: float32 [1024, 128], P('ctx', 'head'), may hold values from 6 to 9
- indexer_query: bfloat16 [1024, 64, 128], P('ctx', 'head'), may hold values from -8 to 8
- indexer_key: bfloat16 [1024, 128], P('ctx'), may hold values from -4 to 4
- indexer_weight: bfloat16 [1024, 64], P('ctx', 'head'), may hold values from -4 to 4
Outputs:
- query_grad: float32 [1024, 64, 128], P('ctx', 'head')
- key_grad: float32 [1024, 128], P(('ctx', 'head'))
The draws below stay inside these ranges and needn't reach their ends.
Inputs may be any that keep to these rules, and one draw needn't show every extreme that they name: `block_order`: entries 2 i and 2 i + 1 are the blocks stored on ctx index i; all entries together are each of 0 to 15 once, and the two entries of one index sum to 15.
All inputs are finite; a program needn't handle non-finite values.
Results may differ from the reference program's by a relative error of at most 0.0037.
Values may be sent and summed in bfloat16 or wider, within the bound.
A program may use at most 128 MiB of HBM per device.

```python
import math
import jax
import jax.numpy as jnp
from jax import lax

HEADS = 128
LATENT = 576
IDX_HEADS = 64
IDX_DIM = 128
HALF = 64
BLOCKS = 16
TOKENS = 1024


def scaled_rows(key, shape, lower, upper):
    return jnp.exp(jax.random.uniform(key, shape, jnp.float32, math.log(lower), math.log(upper)))


def draw_block_order(key, part):
    shuffled = jax.random.permutation(key, BLOCKS // 2).astype(jnp.int32)
    upper_block = BLOCKS - 1 - shuffled
    return jnp.stack((shuffled, upper_block), axis=1).reshape(-1).astype(jnp.int32)


def draw_query_latent(key, part):
    base_key = jax.random.fold_in(key, 21)
    scale_key = jax.random.fold_in(key, 22)
    row_scale = scaled_rows(scale_key, (TOKENS, HEADS, 1), 0.5, 4.0)
    values = jnp.clip(jax.random.normal(base_key, (TOKENS, HEADS, LATENT), jnp.float32), -3.0, 3.0)
    return (values * row_scale).astype(jnp.bfloat16)


def draw_key_latent(key, part):
    base_key = jax.random.fold_in(key, 23)
    scale_key = jax.random.fold_in(key, 24)
    row_scale = scaled_rows(scale_key, (TOKENS, 1), 0.5, 2.0)
    values = jnp.clip(jax.random.normal(base_key, (TOKENS, LATENT), jnp.float32), -3.0, 3.0)
    return (values * row_scale).astype(jnp.bfloat16)


def indexer_draw(key):
    query_key = jax.random.fold_in(key, 31)
    keyset_key = jax.random.fold_in(key, 32)
    weight_key = jax.random.fold_in(key, 33)
    query = jnp.clip(jax.random.normal(query_key, (TOKENS, IDX_HEADS, IDX_DIM), jnp.float32), -4.0, 4.0)
    keyset = jnp.clip(jax.random.normal(keyset_key, (TOKENS, IDX_DIM), jnp.float32), -4.0, 4.0)
    weight = jnp.clip(jax.random.normal(weight_key, (TOKENS, IDX_HEADS), jnp.float32), -4.0, 4.0)
    return (query, keyset, weight)


def draw_indexer_query(key, part):
    return indexer_draw(key)[0].astype(jnp.bfloat16)


def draw_indexer_key(key, part):
    return indexer_draw(key)[1].astype(jnp.bfloat16)


def draw_indexer_weight(key, part):
    return indexer_draw(key)[2].astype(jnp.bfloat16)


def shard_levels(stream_key, extent, split, least, top_value):
    def one(dim, shards_of):
        steps = jax.random.uniform(jax.random.fold_in(jax.random.fold_in(stream_key, 6), dim), (shards_of,), jnp.float32, least / len(split), top_value / len(split))
        return jnp.repeat(jnp.exp(steps), extent[dim] // shards_of).reshape((-1,) + (1,) * (len(extent) - dim - 1))

    factor_of = one(*split[0])
    for cut in split[1:]:
        factor_of = factor_of * one(*cut)
    return factor_of


def setup_inputs(seed: int = 0) -> dict:
    splits = jax.random.split(jax.random.key(seed), 8)
    block_order = draw_block_order(jax.random.fold_in(splits[7], 71), 0)
    query_latent = draw_query_latent(jax.random.fold_in(splits[7], 71), 0)
    key_latent = draw_key_latent(jax.random.fold_in(splits[7], 71), 0)
    normalizer = jnp.clip(6.0 + 3.0 * jax.random.uniform(splits[3], (TOKENS, HEADS), jnp.float32) ** shard_levels(splits[3], (TOKENS, HEADS), ((0, 8), (1, 4)), -0.2, 0.2), 6.0, 9.0)
    indexer_query = draw_indexer_query(jax.random.fold_in(splits[7], 71), 0)
    indexer_key = draw_indexer_key(jax.random.fold_in(splits[7], 71), 0)
    indexer_weight = draw_indexer_weight(jax.random.fold_in(splits[7], 71), 0)
    return {"block_order": block_order, "query_latent": query_latent, "key_latent": key_latent, "normalizer": normalizer, "indexer_query": indexer_query, "indexer_key": indexer_key, "indexer_weight": indexer_weight}


mla_scale = 192.0 ** -0.5
loss_scale = 64.0


def reference(block_order, query_latent, key_latent, normalizer, indexer_query, indexer_key, indexer_weight):
    query_rows = 2 * HALF
    block_count = TOKENS // query_rows
    positions = (block_order[:, None] * HALF + jnp.arange(HALF, dtype=jnp.int32)[None, :]).reshape(-1).astype(jnp.int32)
    kv_float = key_latent.astype(jnp.float32)
    key_float = indexer_key.astype(jnp.float32)
    idx_scale = (IDX_HEADS * IDX_DIM) ** -0.5

    def scan_step(key_accum, pieces):
        query_block, lse_block, idx_block, weight_block, query_pos = pieces
        scores = jnp.einsum('thl,sl->ths', query_block.astype(jnp.float32), kv_float) * mla_scale
        visible = positions[None, :] <= query_pos[:, None]
        target_sum = jnp.where(visible, jnp.sum(jnp.exp(scores - lse_block[:, :, None]), axis=1), 0.0)
        row_total = jnp.sum(target_sum, axis=1, keepdims=True)
        idx_dot = jnp.einsum('tjd,sd->tjs', idx_block.astype(jnp.float32), key_float)
        logits = idx_scale * jnp.sum(weight_block.astype(jnp.float32)[:, :, None] * jnp.maximum(idx_dot, 0.0), axis=1)
        row_top = jnp.max(jnp.where(visible, logits, -jnp.inf), axis=1, keepdims=True)
        exp_logit = jnp.where(visible, jnp.exp(logits - row_top), 0.0)
        norm_sum = jnp.sum(exp_logit, axis=1, keepdims=True)
        grad_logit = jnp.where(visible, loss_scale * (exp_logit / norm_sum - target_sum / row_total), 0.0).astype(jnp.bfloat16)
        weight_scaled = weight_block.astype(jnp.float32) * idx_scale
        coefficient = jnp.where(idx_dot > 0, grad_logit.astype(jnp.float32)[:, None, :] * weight_scaled[:, :, None], 0.0).astype(jnp.bfloat16)
        coeff_float = coefficient.astype(jnp.float32)
        query_part = jnp.einsum('tjs,sd->tjd', coeff_float, key_float)
        key_accum = key_accum + jnp.einsum('tjs,tjd->sd', coeff_float, idx_block.astype(jnp.float32))
        return key_accum, query_part

    pieces = (
        query_latent.reshape(block_count, query_rows, HEADS, LATENT),
        normalizer.reshape(block_count, query_rows, HEADS),
        indexer_query.reshape(block_count, query_rows, IDX_HEADS, IDX_DIM),
        indexer_weight.reshape(block_count, query_rows, IDX_HEADS),
        positions.reshape(block_count, query_rows),
    )
    key_grad, query_parts = lax.scan(scan_step, jnp.zeros((TOKENS, IDX_DIM), jnp.float32), pieces)
    query_grad = query_parts.reshape(TOKENS, IDX_HEADS, IDX_DIM)
    return query_grad, key_grad
```

```python
import functools
import math

import jax
import jax.numpy as jnp
from jax import lax
from jax.experimental import pallas as pl
from jax.experimental.pallas import tpu as pltpu
from jax.sharding import PartitionSpec as P

MESH = pl.DeviceIdType.MESH
mla_scale = 192.0 ** (-0.5)
loss_scale = 64.0
log2e = math.log2(math.e)
NT_DIMS = (((1,), (1,)), ((), ()))


def remote(src, dst, send, recv, device):
    return pltpu.make_async_remote_copy(
        src_ref=src, dst_ref=dst, send_sem=send, recv_sem=recv, device_id=device, device_id_type=MESH
    )


def partner(group, step, groups):
    bit = 1
    while bit < groups:
        if step & bit:
            group = group + bit * (1 - 2 * lax.rem(group // bit, 2))
        bit *= 2
    return group


def kernel(
    groups, shares, order, lat, idx, iq, iw_far, q_far, norm_far, qg_out, kg_out,
    all_lat, all_idx, q, iq_near, iqf, iw, norm, keys, keys_t, coefs, rate,
    lsend, tsend, lrecv, trecv, gall, ksend, krecv, kown, kz, kzr, qg,
    local, ds, dr, fs, fr, xs, xr, gs, gr, ks, kr, zs, zr,
):
    ctx, head = lax.axis_index("ctx"), lax.axis_index("head")
    group, core = ctx // 2, lax.rem(ctx, 2)
    sibling = group * 2 + 1 - core
    blocks = order.shape[0]
    rows, dim = idx.shape
    half = rows // 2
    share = half // shares
    heads, idx_heads = q.shape[0], iw.shape[0]
    bundle = 8
    idx_scale = (idx_heads * shares * dim) ** (-0.5)

    own = [
        pltpu.make_async_copy(iq, iq_near, local.at[0]),
        pltpu.make_async_copy(iw_far, iw, local.at[1]),
        pltpu.make_async_copy(idx, all_idx.at[ctx], local.at[2]),
        pltpu.make_async_copy(lat, all_lat.at[ctx], local.at[3]),
        pltpu.make_async_copy(norm_far, norm, local.at[4]),
        pltpu.make_async_copy(q_far, q, local.at[5]),
    ]
    for copy in own:
        copy.start()
    barrier = pltpu.get_barrier_semaphore()
    for step in range(1, groups):
        peer = partner(group, step, groups) * 2
        for j in range(2):
            pl.semaphore_signal(barrier, 1, device_id={"ctx": peer + j}, device_id_type=MESH)
    pl.semaphore_signal(barrier, 1, device_id={"ctx": sibling}, device_id_type=MESH)
    for step in range(1, shares):
        peer = lax.rem(head + step, shares)
        pl.semaphore_signal(barrier, 1, device_id={"head": peer}, device_id_type=MESH)
    own[0].wait()
    iqf[...] = jnp.swapaxes(iq_near[...], 0, 1).reshape(idx_heads * rows, dim)
    pl.semaphore_wait(barrier, 2 * (groups - 1) + 1 + shares - 1)

    sent = []

    def go(copy):
        copy.start()
        sent.append(copy)

    for k, (src, dst) in enumerate(((idx, all_idx), (lat, all_lat))):
        go(remote(src, dst.at[ctx], fs.at[k, 0], fr.at[k, 0], {"ctx": sibling}))
        for step in range(1, groups):
            peer = partner(group, step, groups) * 2 + core
            go(remote(src, dst.at[ctx], ds.at[k, step], dr.at[k, step], {"ctx": peer}))

    def relay(k, step):
        source = partner(group, step, groups) * 2 + core
        slot = (all_idx, all_lat)[k].at[source]
        remote(slot, slot, ds.at[k, step], dr.at[k, step], {"ctx": sibling}).wait_recv()
        go(remote(slot, slot, fs.at[k, step], fr.at[k, step], {"ctx": sibling}))

    def arrive(k, step):
        slot = (all_idx, all_lat)[k].at[partner(group, step, groups) * 2 + 1 - core]
        remote(slot, slot, fs.at[k, step], fr.at[k, step], {"ctx": sibling}).wait_recv()

    def swapped(c):
        return order[2 * c] >= blocks // 2

    def lowest(c):
        return jnp.minimum(order[2 * c], order[2 * c + 1])

    mine_swapped, mine = swapped(ctx), lowest(ctx)
    lane = lax.broadcasted_iota(jnp.int32, (half, rows), 1)

    def turn(x):
        return pltpu.roll(x, half, 1)

    def pack(total, source):
        total = total.T
        first, second = total[:half], total[half:]
        hi = jnp.where(mine_swapped, first, second)
        lo = jnp.where(mine_swapped, second, first)
        packed, low = [], []
        for j in range(2):
            c = 2 * source + j
            flip, early = swapped(c), lowest(c) < mine
            h, l = hi[:, j * rows : (j + 1) * rows], lo[:, j * rows : (j + 1) * rows]
            a = jnp.where(flip, turn(h), h)
            b = jnp.where(flip, l, turn(l))
            packed.append(jnp.where(early & (lane >= half), b, a))
            low.append(b)
        return jnp.concatenate(packed, axis=1), jnp.where(core == 0, low[0], low[1])

    def unpack(slot, source):
        piece = jnp.concatenate([gall[z, slot] for z in range(shares)], axis=0)
        piece = piece.astype(jnp.float32)
        his, los = [], []
        for j in range(2):
            c = 2 * source + j
            flip, early = swapped(c), lowest(c) < mine
            x = piece[:, j * rows : (j + 1) * rows]
            low_lanes = early & (lane >= half)
            h = jnp.where(low_lanes, 0.0, x)
            l = jnp.where(low_lanes, x, 0.0)
            if slot == 0:
                extra = jnp.concatenate(
                    [gall[z, groups, :, :rows] for z in range(shares)], axis=0
                ).astype(jnp.float32)
                l = jnp.where(core == j, extra, l)
            his.append(jnp.where(flip, turn(h), h))
            los.append(jnp.where(flip, l, turn(l)))
        hi, lo = jnp.concatenate(his, axis=1), jnp.concatenate(los, axis=1)
        first = jnp.where(mine_swapped, hi, lo)
        second = jnp.where(mine_swapped, lo, hi)
        return jnp.concatenate((first, second), axis=0).T

    def exchange(k, slot, width):
        send, recv = ((lsend, lrecv), (tsend, trecv))[k]
        for step in range(1, shares):
            peer = lax.rem(head + step, shares)
            go(
                remote(
                    send.at[peer, slot, :, pl.ds(0, width)],
                    recv.at[step, slot, :, pl.ds(0, width)],
                    xs.at[k, slot, step], xr.at[k, slot, step], {"head": peer},
                )
            )

    def deal(k, slot, packed):
        send = (lsend, tsend)[k]
        for z in range(shares):
            send[z, slot, :, : packed.shape[1]] = packed[z * share : (z + 1) * share].astype(
                send.dtype
            )
        exchange(k, slot, packed.shape[1])

    def logits(step):
        source = partner(group, step, groups)
        chip = jnp.concatenate((all_idx[2 * source], all_idx[2 * source + 1]), axis=0)
        keys_t[:, step * 2 * rows : (step + 1) * 2 * rows] = chip.T
        total = jnp.zeros((2 * rows, rows), jnp.float32)
        for p in range(idx_heads // 2):
            cols = slice(2 * p * rows, 2 * (p + 1) * rows)
            dots = lax.dot_general(
                chip, iqf[cols, :], NT_DIMS, preferred_element_type=jnp.float32
            )
            coefs[step * 2 * rows : (step + 1) * 2 * rows, cols] = jnp.where(
                dots > 0, 1.0, 0.0
            ).astype(jnp.bfloat16)
            dots = jnp.maximum(dots, 0.0)
            total = total + dots[:, :rows] * weights[2 * p : 2 * p + 1]
            total = total + dots[:, rows:] * weights[2 * p + 1 : 2 * p + 2]
        packed, low = pack(total, source)
        deal(0, step, packed)
        if step == 0:
            deal(0, groups, low)

    def score(step):
        source = partner(group, step, groups)
        keys[...] = jnp.concatenate((all_lat[2 * source], all_lat[2 * source + 1]), axis=1).T

        def body(i, total):
            shift = norm[pl.ds(pl.multiple_of(i * bundle, bundle), bundle), :] * log2e
            for h in range(0, bundle, 2):
                pair = jnp.concatenate((q[i * bundle + h], q[i * bundle + h + 1]), axis=1)
                scores = jnp.dot(keys[...], pair, preferred_element_type=jnp.float32) * (
                    mla_scale * log2e
                )
                total = total + jnp.exp2(scores[:, :rows] - shift[h : h + 1])
                total = total + jnp.exp2(scores[:, rows:] - shift[h + 1 : h + 2])
            return total

        total = lax.fori_loop(
            0, heads // bundle, body, jnp.zeros((2 * rows, rows), jnp.float32)
        )
        packed, low = pack(total, source)
        deal(1, step, packed)
        if step == 0:
            deal(1, groups, low)

    own[1].wait()
    weights = iw[...].astype(jnp.float32) * idx_scale
    own[2].wait()
    arrive_own = all_idx.at[sibling]
    remote(arrive_own, arrive_own, fs.at[0, 0], fr.at[0, 0], {"ctx": sibling}).wait_recv()
    logits(0)
    own[3].wait()
    own[4].wait()
    own[5].wait()
    arrive_own = all_lat.at[sibling]
    remote(arrive_own, arrive_own, fs.at[1, 0], fr.at[1, 0], {"ctx": sibling}).wait_recv()
    score(0)
    for step in range(1, groups):
        relay(0, step)
    for step in range(1, groups):
        arrive(0, step)
        logits(step)
        if step < 3:
            relay(1, step)
    for step in range(1, groups):
        arrive(1, step)
        score(step)
        if 2 < step + 2 < groups:
            relay(1, step + 2)

    shape = (share, 2 * rows)
    token = head * share + lax.broadcasted_iota(jnp.int32, shape, 0)
    column = lax.broadcasted_iota(jnp.int32, shape, 1)
    inner = lax.rem(column, rows)
    later = inner >= half

    def columns(slot):
        if slot == groups:
            seen = later & (inner - half <= token)
            return later[:, :rows], seen[:, :rows], rows
        source = partner(group, slot, groups)
        early = [(lowest(2 * source + j) < mine).astype(jnp.int32) for j in range(2)]
        low = later & (jnp.where(column < rows, early[0], early[1]) > 0)
        seen = None
        if slot == 0:
            mixed = (column >= core * rows) & (column < (core + 1) * rows) & later
            seen = jnp.logical_not(mixed) | (inner - half <= token)
        return low, seen, 2 * rows

    slots = [*range(groups - 1, 0, -1), 0, groups]
    table = {slot: columns(slot) for slot in slots}

    def gather_sum(k, slot):
        send, recv = ((lsend, lrecv), (tsend, trecv))[k]
        width = table[slot][2]
        value = send[head, slot, :, :width].astype(jnp.float32)
        for step in range(1, shares):
            piece = recv.at[step, slot, :, pl.ds(0, width)]
            remote(piece, piece, xs.at[k, slot, step], xr.at[k, slot, step], {"head": head}).wait_recv()
            value = value + recv[step, slot, :, :width].astype(jnp.float32)
        return value

    inf = jnp.float32(jnp.inf)

    def split(values, reduce, fill):
        his, los = [], []
        for slot, value in values.items():
            low, seen, _ = table[slot]
            h = low if seen is None else low | jnp.logical_not(seen)
            l = jnp.logical_not(low) if seen is None else jnp.logical_not(low & seen)
            his.append(reduce(jnp.where(h, fill, value), axis=1, keepdims=True))
            los.append(reduce(jnp.where(l, fill, value), axis=1, keepdims=True))
        return his, los

    scored = {slot: gather_sum(0, slot) for slot in slots}
    his, los = split(scored, jnp.max, -inf)
    hi_top, lo_top = functools.reduce(jnp.maximum, his), functools.reduce(jnp.maximum, los)
    scored = {
        slot: jnp.exp(value - jnp.where(table[slot][0], lo_top, hi_top))
        for slot, value in scored.items()
    }
    his, los = split(scored, jnp.sum, 0.0)
    hi_norm, lo_norm = loss_scale / sum(his), loss_scale / sum(los)
    target = {slot: gather_sum(1, slot) for slot in slots}
    his, los = split(target, jnp.sum, 0.0)
    hi_total, lo_total = loss_scale / sum(his), loss_scale / sum(los)
    for slot in slots:
        low, seen, width = table[slot]
        value = scored[slot] * jnp.where(low, lo_norm, hi_norm)
        value = value - target[slot] * jnp.where(low, lo_total, hi_total)
        if seen is not None:
            value = jnp.where(seen, value, 0.0)
        gall[head, slot, :, :width] = value.astype(jnp.bfloat16)
        for step in range(1, shares):
            peer = lax.rem(head + step, shares)
            piece = gall.at[head, slot, :, pl.ds(0, width)]
            go(remote(piece, piece, gs.at[slot, step], gr.at[slot, step], {"head": peer}))

    def granted(slot):
        for step in range(1, shares):
            source = lax.rem(head + shares - step, shares)
            piece = gall.at[source, slot, :, pl.ds(0, table[slot][2])]
            remote(piece, piece, gs.at[slot, step], gr.at[slot, step], {"head": source}).wait_recv()

    for slot in [*range(groups - 1, 0, -1), 0]:
        granted(slot)
        if slot == 0:
            granted(groups)
        source = partner(group, slot, groups)
        rate[...] = unpack(slot, source)
        span = slice(slot * 2 * rows, (slot + 1) * 2 * rows)
        for h in range(idx_heads):
            cols = slice(h * rows, (h + 1) * rows)
            coefs[span, cols] = (rate[...] * weights[h : h + 1]).astype(jnp.bfloat16) * coefs[
                span, cols
            ]
        total = jnp.dot(coefs[span, :], iqf[...], preferred_element_type=jnp.float32)
        if slot == 0:
            kown[...] = total.reshape(2, rows, dim)
        ksend[slot] = total.astype(jnp.bfloat16).reshape(2, rows, dim)
        if slot == 0:
            go(
                remote(
                    ksend.at[0, 1 - core], krecv.at[0, core], ks.at[0, 0], kr.at[0, core],
                    {"ctx": sibling},
                )
            )
        else:
            for j in range(2):
                go(
                    remote(
                        ksend.at[slot, j], krecv.at[slot, core], ks.at[slot, j], kr.at[slot, core],
                        {"ctx": source * 2 + j},
                    )
                )

    def query(p):
        cols = slice(2 * p * rows, 2 * (p + 1) * rows)
        value = jnp.dot(keys_t[...], coefs[:, cols], preferred_element_type=jnp.float32).T
        qg[:, 2 * p, :] = value[:rows]
        qg[:, 2 * p + 1, :] = value[rows:]

    pairs = idx_heads // 2
    for p in range(pairs // 2):
        query(p)
    value = kown[core]
    for slot in [*range(groups - 1, 0, -1), 0]:
        for k in range(2) if slot else (1 - core,):
            piece = krecv.at[slot, k]
            remote(piece, piece, ks.at[slot, 0], kr.at[slot, k], {"ctx": sibling}).wait_recv()
            value = value + krecv[slot, k].astype(jnp.float32)
    kz[...] = value
    part = rows // shares
    for step in range(1, shares):
        peer = lax.rem(head + step, shares)
        take = pl.ds(pl.multiple_of(peer * part, part), part)
        go(remote(kz.at[take], kzr.at[step], zs.at[step], zr.at[step], {"head": peer}))
    for p in range(pairs // 2, pairs):
        query(p)
    out = pltpu.make_async_copy(qg, qg_out, local.at[6])
    out.start()
    value = kz[pl.ds(pl.multiple_of(head * part, part), part), :]
    for step in range(1, shares):
        remote(kzr.at[step], kzr.at[step], zs.at[step], zr.at[step], {"head": head}).wait_recv()
        value = value + kzr[step]
    kg_out[...] = value
    for copy in sent:
        copy.wait_send()
    out.wait()


def per_device(
    block_order, query_latent, key_latent, normalizer, indexer_query, indexer_key, indexer_weight
):
    cycle, shares = lax.axis_size("ctx"), lax.axis_size("head")
    groups = cycle // 2
    rows, dim = indexer_key.shape
    heads, latent = query_latent.shape[1:]
    idx_heads = indexer_query.shape[1]
    share = rows // 2 // shares
    bf16, f32 = jnp.bfloat16, jnp.float32
    dma, vmem = pltpu.SemaphoreType.DMA, pltpu.VMEM
    return pl.pallas_call(
        functools.partial(kernel, groups, shares),
        out_shape=(
            jax.ShapeDtypeStruct((rows, idx_heads, dim), f32),
            jax.ShapeDtypeStruct((rows // shares, dim), f32),
        ),
        in_specs=[pl.BlockSpec(memory_space=pltpu.SMEM)] + [pl.BlockSpec(memory_space=pl.ANY)] * 6,
        out_specs=(pl.BlockSpec(memory_space=pl.ANY), pl.BlockSpec(memory_space=pltpu.VMEM)),
        scratch_shapes=[
            vmem((cycle, latent, rows), bf16),
            vmem((cycle, rows, dim), bf16),
            vmem((heads, latent, rows), bf16),
            vmem((rows, idx_heads, dim), bf16),
            vmem((idx_heads * rows, dim), bf16),
            vmem((idx_heads, rows), bf16),
            vmem((heads, rows), f32),
            vmem((2 * rows, latent), bf16),
            vmem((dim, cycle * rows), bf16),
            vmem((cycle * rows, idx_heads * rows), bf16),
            vmem((2 * rows, rows), f32),
            vmem((shares, groups + 1, share, 2 * rows), f32),
            vmem((shares, groups + 1, share, 2 * rows), bf16),
            vmem((shares, groups + 1, share, 2 * rows), f32),
            vmem((shares, groups + 1, share, 2 * rows), bf16),
            vmem((shares, groups + 1, share, 2 * rows), bf16),
            vmem((groups, 2, rows, dim), bf16),
            vmem((groups, 2, rows, dim), bf16),
            vmem((2, rows, dim), f32),
            vmem((rows, dim), f32),
            vmem((shares, rows // shares, dim), f32),
            vmem((rows, idx_heads, dim), f32),
            dma((7,)),
            dma((2, groups)), dma((2, groups)), dma((2, groups)), dma((2, groups)),
            dma((2, groups + 1, shares)), dma((2, groups + 1, shares)),
            dma((groups + 1, shares)), dma((groups + 1, shares)),
            dma((groups, 2)), dma((groups, 2)),
            dma((shares,)), dma((shares,)),
        ],
        compiler_params=pltpu.CompilerParams(collective_id=0, has_side_effects=True),
        name="indexer",
    )(
        block_order, key_latent.T, indexer_key, indexer_query, indexer_weight.T,
        query_latent.transpose(1, 2, 0), normalizer.T,
    )


def solution(mesh):
    return jax.shard_map(
        per_device,
        mesh=mesh,
        in_specs=(
            P(),
            P("ctx", "head", None),
            P("ctx", None),
            P("ctx", "head"),
            P("ctx", "head", None),
            P("ctx", None),
            P("ctx", "head"),
        ),
        out_specs=(P("ctx", "head", None), P(("ctx", "head"), None)),
        check_vma=False,
    )
```

```python
import functools
import math

import jax
import jax.numpy as jnp
from jax import lax
from jax.experimental import pallas as pl
from jax.experimental.pallas import tpu as pltpu
from jax.sharding import PartitionSpec as P

MESH = pl.DeviceIdType.MESH
mla_scale = 192.0 ** (-0.5)
loss_scale = 64.0
log2e = math.log2(math.e)
NT_DIMS = (((1,), (1,)), ((), ()))


def remote(src, dst, send, recv, device):
    return pltpu.make_async_remote_copy(
        src_ref=src, dst_ref=dst, send_sem=send, recv_sem=recv, device_id=device, device_id_type=MESH
    )


def partner(group, step, groups):
    bit = 1
    while bit < groups:
        if step & bit:
            group = group + bit * (1 - 2 * lax.rem(group // bit, 2))
        bit *= 2
    return group


def kernel(
    groups, shares, order_far, lat, idx, iq, iw_far, q_far, norm_far, qg, kg_out,
    order,
    all_lat, all_idx, q, iq_near, iqf, iw, norm, keys, keys_t, coefs, rate,
    lsend, tsend, lrecv, trecv, gall, ksend, krecv, kown, kz, kzs, kzr,
    local, ds, dr, fs, fr, xs, xr, gs, gr, ks, kr, zs, zr,
):
    ctx, head = lax.axis_index("ctx"), lax.axis_index("head")
    group, core = ctx // 2, lax.rem(ctx, 2)
    sibling = group * 2 + 1 - core
    blocks = order.shape[0]
    rows, dim = idx.shape
    half = rows // 2
    share = half // shares
    heads, idx_heads = q.shape[0], iw.shape[0]
    bundle = 8
    idx_scale = (idx_heads * shares * dim) ** (-0.5)

    own = [
        pltpu.make_async_copy(iq, iq_near, local.at[0]),
        pltpu.make_async_copy(iw_far, iw, local.at[1]),
        pltpu.make_async_copy(idx, all_idx.at[ctx], local.at[2]),
        pltpu.make_async_copy(lat, all_lat.at[ctx], local.at[3]),
        pltpu.make_async_copy(norm_far, norm, local.at[4]),
        pltpu.make_async_copy(q_far, q, local.at[5]),
        pltpu.make_async_copy(order_far, order, local.at[6]),
    ]
    barrier = pltpu.get_barrier_semaphore()
    for step in range(1, groups):
        peer = partner(group, step, groups) * 2
        for j in range(2):
            pl.semaphore_signal(barrier, 1, device_id={"ctx": peer + j}, device_id_type=MESH)
    pl.semaphore_signal(barrier, 1, device_id={"ctx": sibling}, device_id_type=MESH)
    for step in range(1, shares):
        peer = lax.rem(head + step, shares)
        pl.semaphore_signal(barrier, 1, device_id={"head": peer}, device_id_type=MESH)
    for copy in own:
        copy.start()
    pl.semaphore_wait(barrier, 2 * (groups - 1) + 1 + shares - 1)

    sent = []

    def go(copy):
        copy.start()
        sent.append(copy)

    for k, (src, dst) in enumerate(((idx, all_idx), (lat, all_lat))):
        go(remote(src, dst.at[ctx], fs.at[k, 0], fr.at[k, 0], {"ctx": sibling}))
        for step in range(1, groups):
            peer = partner(group, step, groups) * 2 + core
            go(remote(src, dst.at[ctx], ds.at[k, step], dr.at[k, step], {"ctx": peer}))

    def relay(k, step):
        source = partner(group, step, groups) * 2 + core
        slot = (all_idx, all_lat)[k].at[source]
        remote(slot, slot, ds.at[k, step], dr.at[k, step], {"ctx": sibling}).wait_recv()
        go(remote(slot, slot, fs.at[k, step], fr.at[k, step], {"ctx": sibling}))

    def arrive(k, step):
        slot = (all_idx, all_lat)[k].at[partner(group, step, groups) * 2 + 1 - core]
        remote(slot, slot, fs.at[k, step], fr.at[k, step], {"ctx": sibling}).wait_recv()

    def swapped(c):
        return order[2 * c] >= blocks // 2

    def lowest(c):
        return jnp.minimum(order[2 * c], order[2 * c + 1])

    own[6].wait()
    mine_swapped, mine = swapped(ctx), lowest(ctx)
    lane = lax.broadcasted_iota(jnp.int32, (half, rows), 1)

    def turn(x):
        return pltpu.roll(x, half, 1)

    def pack(total, source):
        total = total.T
        first, second = total[:half], total[half:]
        hi = jnp.where(mine_swapped, first, second)
        lo = jnp.where(mine_swapped, second, first)
        packed, low = [], []
        for j in range(2):
            c = 2 * source + j
            flip, early = swapped(c), lowest(c) < mine
            h, l = hi[:, j * rows : (j + 1) * rows], lo[:, j * rows : (j + 1) * rows]
            a = jnp.where(flip, turn(h), h)
            b = jnp.where(flip, l, turn(l))
            packed.append(jnp.where(early & (lane >= half), b, a))
            low.append(b)
        return jnp.concatenate(packed, axis=1), jnp.where(core == 0, low[0], low[1])

    def unpack(slot, source):
        piece = jnp.concatenate([gall[z, slot] for z in range(shares)], axis=0)
        piece = piece.astype(jnp.float32)
        his, los = [], []
        for j in range(2):
            c = 2 * source + j
            flip, early = swapped(c), lowest(c) < mine
            x = piece[:, j * rows : (j + 1) * rows]
            low_lanes = early & (lane >= half)
            h = jnp.where(low_lanes, 0.0, x)
            l = jnp.where(low_lanes, x, 0.0)
            if slot == 0:
                extra = jnp.concatenate(
                    [gall[z, groups, :, :rows] for z in range(shares)], axis=0
                ).astype(jnp.float32)
                l = jnp.where(core == j, extra, l)
            his.append(jnp.where(flip, turn(h), h))
            los.append(jnp.where(flip, l, turn(l)))
        hi, lo = jnp.concatenate(his, axis=1), jnp.concatenate(los, axis=1)
        first = jnp.where(mine_swapped, hi, lo)
        second = jnp.where(mine_swapped, lo, hi)
        return jnp.concatenate((first, second), axis=0).T

    def exchange(k, slot, width):
        send, recv = ((lsend, lrecv), (tsend, trecv))[k]
        for step in range(1, shares):
            peer = lax.rem(head + step, shares)
            go(
                remote(
                    send.at[peer, slot, :, pl.ds(0, width)],
                    recv.at[step, slot, :, pl.ds(0, width)],
                    xs.at[k, slot, step], xr.at[k, slot, step], {"head": peer},
                )
            )

    def deal(k, slot, packed):
        send = (lsend, tsend)[k]
        for z in range(shares):
            send[z, slot, :, : packed.shape[1]] = packed[z * share : (z + 1) * share].astype(
                send.dtype
            )
        exchange(k, slot, packed.shape[1])

    def logits(step):
        source = partner(group, step, groups)
        chip = jnp.concatenate((all_idx[2 * source], all_idx[2 * source + 1]), axis=0)
        keys_t[:, step * 2 * rows : (step + 1) * 2 * rows] = chip.T
        total = jnp.zeros((2 * rows, rows), jnp.float32)
        for p in range(idx_heads // 2):
            cols = slice(2 * p * rows, 2 * (p + 1) * rows)
            dots = lax.dot_general(
                chip, iqf[cols, :], NT_DIMS, preferred_element_type=jnp.float32
            )
            coefs[step * 2 * rows : (step + 1) * 2 * rows, cols] = jnp.where(
                dots > 0, 1.0, 0.0
            ).astype(jnp.bfloat16)
            dots = jnp.maximum(dots, 0.0)
            total = total + dots[:, :rows] * weights[2 * p : 2 * p + 1]
            total = total + dots[:, rows:] * weights[2 * p + 1 : 2 * p + 2]
        packed, low = pack(total, source)
        deal(0, step, packed)
        if step == 0:
            deal(0, groups, low)

    def attend(lhs):
        total = jnp.zeros((lhs.shape[0], rows), jnp.float32)
        for h in range(0, heads, 2):
            pair = jnp.concatenate((q[h], q[h + 1]), axis=1)
            scores = jnp.dot(lhs[...], pair, preferred_element_type=jnp.float32) * (
                mla_scale * log2e
            )
            shift = norm[h : h + 2, :] * log2e
            total = total + jnp.exp2(scores[:, :rows] - shift[:1])
            total = total + jnp.exp2(scores[:, rows:] - shift[1:])
        return total

    def score(step):
        source = partner(group, step, groups)
        if step < groups - 1:
            arrive(1, step)
            keys[...] = jnp.concatenate((all_lat[2 * source], all_lat[2 * source + 1]), axis=1).T
            total = attend(keys)
        else:
            parts = []
            for k, device in enumerate((2 * source + core, 2 * source + 1 - core)):
                if k:
                    arrive(1, step)
                half_keys = keys.at[pl.ds(k * rows, rows)]
                half_keys[...] = all_lat[device].T
                parts.append(attend(half_keys))
            near, other = parts
            total = jnp.concatenate(
                (jnp.where(core == 0, near, other), jnp.where(core == 0, other, near)), axis=0
            )
        packed, low = pack(total, source)
        deal(1, step, packed)
        if step == 0:
            deal(1, groups, low)

    own[0].wait()
    iqf[...] = jnp.swapaxes(iq_near[...], 0, 1).reshape(idx_heads * rows, dim)
    own[1].wait()
    weights = iw[...].astype(jnp.float32) * idx_scale
    own[2].wait()
    arrive(0, 0)
    logits(0)
    for copy in own[3:6]:
        copy.wait()
    score(0)
    for step in range(1, groups):
        relay(0, step)
    for step in range(1, groups):
        arrive(0, step)
        logits(step)
    for step in range(1, min(3, groups)):
        relay(1, step)
    for step in range(1, groups):
        score(step)
        if step + 2 < groups:
            relay(1, step + 2)

    shape = (share, 2 * rows)
    token = head * share + lax.broadcasted_iota(jnp.int32, shape, 0)
    column = lax.broadcasted_iota(jnp.int32, shape, 1)
    inner = lax.rem(column, rows)
    later = inner >= half

    def columns(slot):
        if slot == groups:
            seen = later & (inner - half <= token)
            return later[:, :rows], seen[:, :rows], rows
        source = partner(group, slot, groups)
        early = [(lowest(2 * source + j) < mine).astype(jnp.int32) for j in range(2)]
        low = later & (jnp.where(column < rows, early[0], early[1]) > 0)
        seen = None
        if slot == 0:
            mixed = (column >= core * rows) & (column < (core + 1) * rows) & later
            seen = jnp.logical_not(mixed) | (inner - half <= token)
        return low, seen, 2 * rows

    slots = [*range(groups - 1, 0, -1), 0, groups]
    table = {slot: columns(slot) for slot in slots}

    def gather_sum(k, slot):
        send, recv = ((lsend, lrecv), (tsend, trecv))[k]
        width = table[slot][2]
        value = send[head, slot, :, :width].astype(jnp.float32)
        for step in range(1, shares):
            piece = recv.at[step, slot, :, pl.ds(0, width)]
            remote(piece, piece, xs.at[k, slot, step], xr.at[k, slot, step], {"head": head}).wait_recv()
            value = value + recv[step, slot, :, :width].astype(jnp.float32)
        return value

    inf = jnp.float32(jnp.inf)

    def split(values, reduce, fill):
        his, los = [], []
        for slot, value in values.items():
            low, seen, _ = table[slot]
            h = low if seen is None else low | jnp.logical_not(seen)
            l = jnp.logical_not(low) if seen is None else jnp.logical_not(low & seen)
            his.append(reduce(jnp.where(h, fill, value), axis=1, keepdims=True))
            los.append(reduce(jnp.where(l, fill, value), axis=1, keepdims=True))
        return his, los

    scored = {slot: gather_sum(0, slot) for slot in slots}
    his, los = split(scored, jnp.max, -inf)
    hi_top, lo_top = functools.reduce(jnp.maximum, his), functools.reduce(jnp.maximum, los)
    scored = {
        slot: jnp.exp(value - jnp.where(table[slot][0], lo_top, hi_top))
        for slot, value in scored.items()
    }
    his, los = split(scored, jnp.sum, 0.0)
    hi_norm, lo_norm = loss_scale / sum(his), loss_scale / sum(los)
    target = {slot: gather_sum(1, slot) for slot in slots}
    his, los = split(target, jnp.sum, 0.0)
    hi_total, lo_total = loss_scale / sum(his), loss_scale / sum(los)
    for slot in slots:
        low, seen, width = table[slot]
        value = scored[slot] * jnp.where(low, lo_norm, hi_norm)
        value = value - target[slot] * jnp.where(low, lo_total, hi_total)
        if seen is not None:
            value = jnp.where(seen, value, 0.0)
        gall[head, slot, :, :width] = value.astype(jnp.bfloat16)
        for step in range(1, shares):
            peer = lax.rem(head + step, shares)
            piece = gall.at[head, slot, :, pl.ds(0, width)]
            go(remote(piece, piece, gs.at[slot, step], gr.at[slot, step], {"head": peer}))

    def granted(slot):
        for step in range(1, shares):
            source = lax.rem(head + shares - step, shares)
            piece = gall.at[source, slot, :, pl.ds(0, table[slot][2])]
            remote(piece, piece, gs.at[slot, step], gr.at[slot, step], {"head": source}).wait_recv()

    for slot in [*range(groups - 1, 0, -1), 0]:
        granted(slot)
        if slot == 0:
            granted(groups)
        source = partner(group, slot, groups)
        rate[...] = unpack(slot, source)
        span = slice(slot * 2 * rows, (slot + 1) * 2 * rows)
        for h in range(idx_heads):
            cols = slice(h * rows, (h + 1) * rows)
            coefs[span, cols] = (rate[...] * weights[h : h + 1]).astype(jnp.bfloat16) * coefs[
                span, cols
            ]
        total = jnp.dot(coefs[span, :], iqf[...], preferred_element_type=jnp.float32)
        if slot == 0:
            kown[...] = total.reshape(2, rows, dim)
        ksend[slot] = total.astype(jnp.bfloat16).reshape(2, rows, dim)
        if slot == 0:
            go(
                remote(
                    ksend.at[0, 1 - core], krecv.at[0, core], ks.at[0, 0], kr.at[0, core],
                    {"ctx": sibling},
                )
            )
        else:
            for j in range(2):
                go(
                    remote(
                        ksend.at[slot, j], krecv.at[slot, core], ks.at[slot, j], kr.at[slot, core],
                        {"ctx": source * 2 + j},
                    )
                )

    def query(p):
        cols = slice(2 * p * rows, 2 * (p + 1) * rows)
        value = jnp.dot(keys_t[...], coefs[:, cols], preferred_element_type=jnp.float32).T
        qg[:, 2 * p, :] = value[:rows]
        qg[:, 2 * p + 1, :] = value[rows:]

    pairs = idx_heads // 2
    for p in range(pairs // 2):
        query(p)
    value = kown[core]
    for slot in [*range(groups - 1, 0, -1), 0]:
        for k in range(2) if slot else (1 - core,):
            piece = krecv.at[slot, k]
            remote(piece, piece, ks.at[slot, 0], kr.at[slot, k], {"ctx": sibling}).wait_recv()
            value = value + krecv[slot, k].astype(jnp.float32)
    kz[...] = value
    kzs[...] = value.astype(jnp.bfloat16)
    part = rows // shares
    for step in range(1, shares):
        peer = lax.rem(head + step, shares)
        take = pl.ds(pl.multiple_of(peer * part, part), part)
        go(remote(kzs.at[take], kzr.at[step], zs.at[step], zr.at[step], {"head": peer}))
    for p in range(pairs // 2, pairs):
        query(p)
    value = kz[pl.ds(pl.multiple_of(head * part, part), part), :]
    for step in range(1, shares):
        remote(kzr.at[step], kzr.at[step], zs.at[step], zr.at[step], {"head": head}).wait_recv()
        value = value + kzr[step].astype(jnp.float32)
    kg_out[...] = value
    for copy in sent:
        copy.wait_send()


def per_device(
    block_order, query_latent, key_latent, normalizer, indexer_query, indexer_key, indexer_weight
):
    cycle, shares = lax.axis_size("ctx"), lax.axis_size("head")
    groups = cycle // 2
    rows, dim = indexer_key.shape
    heads, latent = query_latent.shape[1:]
    idx_heads = indexer_query.shape[1]
    share = rows // 2 // shares
    bf16, f32 = jnp.bfloat16, jnp.float32
    dma, vmem = pltpu.SemaphoreType.DMA, pltpu.VMEM
    return pl.pallas_call(
        functools.partial(kernel, groups, shares),
        out_shape=(
            vmem((rows, idx_heads, dim), f32),
            vmem((rows // shares, dim), f32),
        ),
        in_specs=[pl.BlockSpec(memory_space=pl.ANY)] * 7,
        out_specs=(pl.BlockSpec(memory_space=pltpu.VMEM),) * 2,
        scratch_shapes=[
            pltpu.SMEM(block_order.shape, block_order.dtype),
            vmem((cycle, latent, rows), bf16),
            vmem((cycle, rows, dim), bf16),
            vmem((heads, latent, rows), bf16),
            vmem((rows, idx_heads, dim), bf16),
            vmem((idx_heads * rows, dim), bf16),
            vmem((idx_heads, rows), bf16),
            vmem((heads, rows), f32),
            vmem((2 * rows, latent), bf16),
            vmem((dim, cycle * rows), bf16),
            vmem((cycle * rows, idx_heads * rows), bf16),
            vmem((2 * rows, rows), f32),
            vmem((shares, groups + 1, share, 2 * rows), f32),
            vmem((shares, groups + 1, share, 2 * rows), bf16),
            vmem((shares, groups + 1, share, 2 * rows), f32),
            vmem((shares, groups + 1, share, 2 * rows), bf16),
            vmem((shares, groups + 1, share, 2 * rows), bf16),
            vmem((groups, 2, rows, dim), bf16),
            vmem((groups, 2, rows, dim), bf16),
            vmem((2, rows, dim), f32),
            vmem((rows, dim), f32),
            vmem((rows, dim), bf16),
            vmem((shares, rows // shares, dim), bf16),
            dma((7,)),
            dma((2, groups)), dma((2, groups)), dma((2, groups)), dma((2, groups)),
            dma((2, groups + 1, shares)), dma((2, groups + 1, shares)),
            dma((groups + 1, shares)), dma((groups + 1, shares)),
            dma((groups, 2)), dma((groups, 2)),
            dma((shares,)), dma((shares,)),
        ],
        compiler_params=pltpu.CompilerParams(collective_id=0, has_side_effects=True),
        name="indexer",
    )(
        block_order, key_latent.T, indexer_key, indexer_query, indexer_weight.T,
        query_latent.transpose(1, 2, 0), normalizer.T,
    )


def solution(mesh):
    return jax.shard_map(
        per_device,
        mesh=mesh,
        in_specs=(
            P(),
            P("ctx", "head", None),
            P("ctx", None),
            P("ctx", "head"),
            P("ctx", "head", None),
            P("ctx", None),
            P("ctx", "head"),
        ),
        out_specs=(P("ctx", "head", None), P(("ctx", "head"), None)),
        check_vma=False,
    )
```

```python
import functools
import math

import jax
import jax.numpy as jnp
from jax import lax
from jax.experimental import pallas as pl
from jax.experimental.pallas import tpu as pltpu
from jax.sharding import PartitionSpec as P

MESH = pl.DeviceIdType.MESH
mla_scale = 192.0 ** (-0.5)
loss_scale = 64.0
log2e = math.log2(math.e)
NT_DIMS = (((1,), (1,)), ((), ()))


def remote(src, dst, send, recv, device):
    return pltpu.make_async_remote_copy(
        src_ref=src, dst_ref=dst, send_sem=send, recv_sem=recv, device_id=device, device_id_type=MESH
    )


def partner(group, step, groups):
    bit = 1
    while bit < groups:
        if step & bit:
            group = group + bit * (1 - 2 * lax.rem(group // bit, 2))
        bit *= 2
    return group


def kernel(
    groups, shares, order_far, lat, idx, iq, iw_far, q_far, norm_far, qg, kg_out,
    order,
    all_lat, all_idx, q, iq_near, iqf, iw, norm, keys, keys_t, coefs, rate,
    lsend, tsend, lrecv, trecv, gall, ksend, krecv, kown, kz, kzs, kzr,
    local, ds, dr, fs, fr, xs, xr, gs, gr, ks, kr, zs, zr,
):
    ctx, head = lax.axis_index("ctx"), lax.axis_index("head")
    group, core = ctx // 2, lax.rem(ctx, 2)
    sibling = group * 2 + 1 - core
    blocks = order.shape[0]
    rows, dim = idx.shape
    half = rows // 2
    share = half // shares
    heads, idx_heads = q.shape[0], iw.shape[0]
    bundle = 8
    idx_scale = (idx_heads * shares * dim) ** (-0.5)

    own = [
        pltpu.make_async_copy(iq, iq_near, local.at[0]),
        pltpu.make_async_copy(iw_far, iw, local.at[1]),
        pltpu.make_async_copy(idx, all_idx.at[ctx], local.at[2]),
        pltpu.make_async_copy(lat, all_lat.at[ctx], local.at[3]),
        pltpu.make_async_copy(norm_far, norm, local.at[4]),
        pltpu.make_async_copy(q_far, q, local.at[5]),
        pltpu.make_async_copy(order_far, order, local.at[6]),
    ]
    barrier = pltpu.get_barrier_semaphore()
    for step in range(1, groups):
        peer = partner(group, step, groups) * 2
        for j in range(2):
            pl.semaphore_signal(barrier, 1, device_id={"ctx": peer + j}, device_id_type=MESH)
    pl.semaphore_signal(barrier, 1, device_id={"ctx": sibling}, device_id_type=MESH)
    for step in range(1, shares):
        peer = partner(head, step, shares)
        pl.semaphore_signal(barrier, 1, device_id={"head": peer}, device_id_type=MESH)
    for copy in own:
        copy.start()
    pl.semaphore_wait(barrier, 2 * (groups - 1) + 1 + shares - 1)

    sent = []

    def go(copy):
        copy.start()
        sent.append(copy)

    def spread(k, step):
        src, dst = ((idx, all_idx), (lat, all_lat))[k]
        if step:
            peer = partner(group, step, groups) * 2 + core
            go(remote(src, dst.at[ctx], ds.at[k, step], dr.at[k, step], {"ctx": peer}))
        else:
            go(remote(src, dst.at[ctx], fs.at[k, 0], fr.at[k, 0], {"ctx": sibling}))

    near = min(3, groups)
    for k in range(2):
        spread(k, 0)
    for k in range(2):
        for step in range(1, near):
            spread(k, step)
    for step in range(near, groups):
        for k in range(2):
            spread(k, step)

    def relay(k, step):
        source = partner(group, step, groups) * 2 + core
        slot = (all_idx, all_lat)[k].at[source]
        remote(slot, slot, ds.at[k, step], dr.at[k, step], {"ctx": sibling}).wait_recv()
        go(remote(slot, slot, fs.at[k, step], fr.at[k, step], {"ctx": sibling}))

    def arrive(k, step):
        slot = (all_idx, all_lat)[k].at[partner(group, step, groups) * 2 + 1 - core]
        remote(slot, slot, fs.at[k, step], fr.at[k, step], {"ctx": sibling}).wait_recv()

    def swapped(c):
        return order[2 * c] >= blocks // 2

    def lowest(c):
        return jnp.minimum(order[2 * c], order[2 * c + 1])

    own[6].wait()
    mine_swapped, mine = swapped(ctx), lowest(ctx)
    lane = lax.broadcasted_iota(jnp.int32, (half, rows), 1)

    def turn(x):
        return pltpu.roll(x, half, 1)

    def pack(total, source):
        total = total.T
        first, second = total[:half], total[half:]
        hi = jnp.where(mine_swapped, first, second)
        lo = jnp.where(mine_swapped, second, first)
        packed, low = [], []
        for j in range(2):
            c = 2 * source + j
            flip, early = swapped(c), lowest(c) < mine
            h, l = hi[:, j * rows : (j + 1) * rows], lo[:, j * rows : (j + 1) * rows]
            a = jnp.where(flip, turn(h), h)
            b = jnp.where(flip, l, turn(l))
            packed.append(jnp.where(early & (lane >= half), b, a))
            low.append(b)
        return jnp.concatenate(packed, axis=1), jnp.where(core == 0, low[0], low[1])

    def unpack(slot, source):
        piece = jnp.concatenate([gall[z, slot] for z in range(shares)], axis=0)
        piece = piece.astype(jnp.float32)
        his, los = [], []
        for j in range(2):
            c = 2 * source + j
            flip, early = swapped(c), lowest(c) < mine
            x = piece[:, j * rows : (j + 1) * rows]
            low_lanes = early & (lane >= half)
            h = jnp.where(low_lanes, 0.0, x)
            l = jnp.where(low_lanes, x, 0.0)
            if slot == 0:
                extra = jnp.concatenate(
                    [gall[z, groups, :, :rows] for z in range(shares)], axis=0
                ).astype(jnp.float32)
                l = jnp.where(core == j, extra, l)
            his.append(jnp.where(flip, turn(h), h))
            los.append(jnp.where(flip, l, turn(l)))
        hi, lo = jnp.concatenate(his, axis=1), jnp.concatenate(los, axis=1)
        first = jnp.where(mine_swapped, hi, lo)
        second = jnp.where(mine_swapped, lo, hi)
        return jnp.concatenate((first, second), axis=0).T

    def exchange(k, slot, width):
        send, recv = ((lsend, lrecv), (tsend, trecv))[k]
        for step in range(shares - 1, 0, -1):
            peer = partner(head, step, shares)
            go(
                remote(
                    send.at[peer, slot, :, pl.ds(0, width)],
                    recv.at[step, slot, :, pl.ds(0, width)],
                    xs.at[k, slot, step], xr.at[k, slot, step], {"head": peer},
                )
            )

    def deal(k, slot, packed):
        send = (lsend, tsend)[k]
        for z in range(shares):
            send[z, slot, :, : packed.shape[1]] = packed[z * share : (z + 1) * share].astype(
                send.dtype
            )
        exchange(k, slot, packed.shape[1])

    def logits(step):
        source = partner(group, step, groups)
        chip = jnp.concatenate((all_idx[2 * source], all_idx[2 * source + 1]), axis=0)
        keys_t[:, step * 2 * rows : (step + 1) * 2 * rows] = chip.T
        total = jnp.zeros((2 * rows, rows), jnp.float32)
        for p in range(idx_heads // 2):
            cols = slice(2 * p * rows, 2 * (p + 1) * rows)
            dots = lax.dot_general(
                chip, iqf[cols, :], NT_DIMS, preferred_element_type=jnp.float32
            )
            coefs[step * 2 * rows : (step + 1) * 2 * rows, cols] = jnp.where(
                dots > 0, 1.0, 0.0
            ).astype(jnp.bfloat16)
            dots = jnp.maximum(dots, 0.0)
            total = total + dots[:, :rows] * weights[2 * p : 2 * p + 1]
            total = total + dots[:, rows:] * weights[2 * p + 1 : 2 * p + 2]
        packed, low = pack(total, source)
        deal(0, step, packed)
        if step == 0:
            deal(0, groups, low)

    def attend(lhs):
        total = jnp.zeros((lhs.shape[0], rows), jnp.float32)
        for h in range(0, heads, 2):
            pair = jnp.concatenate((q[h], q[h + 1]), axis=1)
            scores = jnp.dot(lhs[...], pair, preferred_element_type=jnp.float32) * (
                mla_scale * log2e
            )
            shift = norm[h : h + 2, :] * log2e
            total = total + jnp.exp2(scores[:, :rows] - shift[:1])
            total = total + jnp.exp2(scores[:, rows:] - shift[1:])
        return total

    def score(step, split):
        source = partner(group, step, groups)
        if split:
            parts = []
            for k, device in enumerate((2 * source + core, 2 * source + 1 - core)):
                if k:
                    arrive(1, step)
                half_keys = keys.at[pl.ds(k * rows, rows)]
                half_keys[...] = all_lat[device].T
                parts.append(attend(half_keys))
            total = jnp.concatenate(
                (jnp.where(core == 0, *parts), jnp.where(core == 0, *parts[::-1])), axis=0
            )
        else:
            arrive(1, step)
            keys[...] = jnp.concatenate((all_lat[2 * source], all_lat[2 * source + 1]), axis=1).T
            total = attend(keys)
        packed, low = pack(total, source)
        deal(1, step, packed)
        if step == 0:
            deal(1, groups, low)

    own[0].wait()
    iqf[...] = jnp.swapaxes(iq_near[...], 0, 1).reshape(idx_heads * rows, dim)
    own[1].wait()
    weights = iw[...].astype(jnp.float32) * idx_scale
    own[2].wait()
    arrive(0, 0)
    logits(0)
    for step in range(1, near):
        relay(0, step)
    for copy in own[3:6]:
        copy.wait()
    score(0, False)
    for step in range(1, near):
        arrive(0, step)
        logits(step)
    for step in range(1, near):
        relay(1, step)
    for step in range(1, groups):
        if near <= step + 1 < groups:
            relay(0, step + 1)
        if step >= near:
            arrive(0, step)
            logits(step)
            relay(1, step)
        score(step, step != near - 1)

    shape = (share, 2 * rows)
    token = head * share + lax.broadcasted_iota(jnp.int32, shape, 0)
    column = lax.broadcasted_iota(jnp.int32, shape, 1)
    inner = lax.rem(column, rows)
    later = inner >= half

    def columns(slot):
        if slot == groups:
            seen = later & (inner - half <= token)
            return later[:, :rows], seen[:, :rows], rows
        source = partner(group, slot, groups)
        early = [(lowest(2 * source + j) < mine).astype(jnp.int32) for j in range(2)]
        low = later & (jnp.where(column < rows, early[0], early[1]) > 0)
        seen = None
        if slot == 0:
            mixed = (column >= core * rows) & (column < (core + 1) * rows) & later
            seen = jnp.logical_not(mixed) | (inner - half <= token)
        return low, seen, 2 * rows

    slots = [*range(groups - 1, 0, -1), 0, groups]
    table = {slot: columns(slot) for slot in slots}

    def gather_sum(k, slot):
        send, recv = ((lsend, lrecv), (tsend, trecv))[k]
        width = table[slot][2]
        value = send[head, slot, :, :width].astype(jnp.float32)
        for step in range(1, shares):
            piece = recv.at[step, slot, :, pl.ds(0, width)]
            remote(piece, piece, xs.at[k, slot, step], xr.at[k, slot, step], {"head": head}).wait_recv()
            value = value + recv[step, slot, :, :width].astype(jnp.float32)
        return value

    inf = jnp.float32(jnp.inf)

    def split(values, reduce, fill):
        his, los = [], []
        for slot, value in values.items():
            low, seen, _ = table[slot]
            h = low if seen is None else low | jnp.logical_not(seen)
            l = jnp.logical_not(low) if seen is None else jnp.logical_not(low & seen)
            his.append(reduce(jnp.where(h, fill, value), axis=1, keepdims=True))
            los.append(reduce(jnp.where(l, fill, value), axis=1, keepdims=True))
        return his, los

    scored = {slot: gather_sum(0, slot) for slot in slots}
    his, los = split(scored, jnp.max, -inf)
    hi_top, lo_top = functools.reduce(jnp.maximum, his), functools.reduce(jnp.maximum, los)
    scored = {
        slot: jnp.exp(value - jnp.where(table[slot][0], lo_top, hi_top))
        for slot, value in scored.items()
    }
    his, los = split(scored, jnp.sum, 0.0)
    hi_norm, lo_norm = loss_scale / sum(his), loss_scale / sum(los)
    target = {slot: gather_sum(1, slot) for slot in slots}
    his, los = split(target, jnp.sum, 0.0)
    hi_total, lo_total = loss_scale / sum(his), loss_scale / sum(los)
    for slot in slots:
        low, seen, width = table[slot]
        value = scored[slot] * jnp.where(low, lo_norm, hi_norm)
        value = value - target[slot] * jnp.where(low, lo_total, hi_total)
        if seen is not None:
            value = jnp.where(seen, value, 0.0)
        gall[head, slot, :, :width] = value.astype(jnp.bfloat16)
        for step in range(shares - 1, 0, -1):
            peer = partner(head, step, shares)
            piece = gall.at[head, slot, :, pl.ds(0, width)]
            go(remote(piece, piece, gs.at[slot, step], gr.at[slot, step], {"head": peer}))

    def granted(slot):
        for step in range(1, shares):
            source = partner(head, step, shares)
            piece = gall.at[source, slot, :, pl.ds(0, table[slot][2])]
            remote(piece, piece, gs.at[slot, step], gr.at[slot, step], {"head": source}).wait_recv()

    for slot in [*range(groups - 1, 0, -1), 0]:
        granted(slot)
        if slot == 0:
            granted(groups)
        source = partner(group, slot, groups)
        rate[...] = unpack(slot, source)
        span = slice(slot * 2 * rows, (slot + 1) * 2 * rows)
        total = jnp.zeros((2 * rows, dim), jnp.float32)
        for p in range(idx_heads // 2):
            cols = slice(2 * p * rows, 2 * (p + 1) * rows)
            value = jnp.concatenate(
                [rate[...] * weights[h : h + 1] for h in (2 * p, 2 * p + 1)], axis=1
            ).astype(jnp.bfloat16) * coefs[span, cols]
            coefs[span, cols] = value
            total = total + jnp.dot(value, iqf[cols, :], preferred_element_type=jnp.float32)
        if slot == 0:
            kown[...] = total.reshape(2, rows, dim)
        ksend[slot] = total.astype(jnp.bfloat16).reshape(2, rows, dim)
        if slot == 0:
            go(
                remote(
                    ksend.at[0, 1 - core], krecv.at[0, core], ks.at[0, 0], kr.at[0, core],
                    {"ctx": sibling},
                )
            )
        else:
            for j in range(2):
                go(
                    remote(
                        ksend.at[slot, j], krecv.at[slot, core], ks.at[slot, j], kr.at[slot, core],
                        {"ctx": source * 2 + j},
                    )
                )

    def query(p):
        cols = slice(2 * p * rows, 2 * (p + 1) * rows)
        value = jnp.dot(keys_t[...], coefs[:, cols], preferred_element_type=jnp.float32).T
        qg[:, 2 * p, :] = value[:rows]
        qg[:, 2 * p + 1, :] = value[rows:]

    pairs = idx_heads // 2
    for p in range(pairs // 2):
        query(p)
    value = kown[core]
    for slot in [*range(groups - 1, 0, -1), 0]:
        for k in range(2) if slot else (1 - core,):
            piece = krecv.at[slot, k]
            remote(piece, piece, ks.at[slot, 0], kr.at[slot, k], {"ctx": sibling}).wait_recv()
            value = value + krecv[slot, k].astype(jnp.float32)
    kz[...] = value
    kzs[...] = value.astype(jnp.bfloat16)
    part = rows // shares
    for step in range(shares - 1, 0, -1):
        peer = partner(head, step, shares)
        take = pl.ds(pl.multiple_of(peer * part, part), part)
        go(remote(kzs.at[take], kzr.at[step], zs.at[step], zr.at[step], {"head": peer}))
    for p in range(pairs // 2, pairs):
        query(p)
    value = kz[pl.ds(pl.multiple_of(head * part, part), part), :]
    for step in range(1, shares):
        remote(kzr.at[step], kzr.at[step], zs.at[step], zr.at[step], {"head": head}).wait_recv()
        value = value + kzr[step].astype(jnp.float32)
    kg_out[...] = value
    for copy in sent:
        copy.wait_send()


def store(qg, kg, qg_out, kg_out, sems):
    copies = [
        pltpu.make_async_copy(qg, qg_out, sems.at[0]), pltpu.make_async_copy(kg, kg_out, sems.at[1])
    ]
    for copy in copies:
        copy.start()
    for copy in copies:
        copy.wait()


def per_device(
    block_order, query_latent, key_latent, normalizer, indexer_query, indexer_key, indexer_weight
):
    cycle, shares = lax.axis_size("ctx"), lax.axis_size("head")
    groups = cycle // 2
    rows, dim = indexer_key.shape
    heads, latent = query_latent.shape[1:]
    idx_heads = indexer_query.shape[1]
    share = rows // 2 // shares
    bf16, f32 = jnp.bfloat16, jnp.float32
    dma, vmem = pltpu.SemaphoreType.DMA, pltpu.VMEM
    results = pl.pallas_call(
        functools.partial(kernel, groups, shares),
        out_shape=(
            vmem((rows, idx_heads, dim), f32),
            vmem((rows // shares, dim), f32),
        ),
        in_specs=[pl.BlockSpec(memory_space=pl.ANY)] * 7,
        out_specs=(pl.BlockSpec(memory_space=pltpu.VMEM),) * 2,
        scratch_shapes=[
            pltpu.SMEM(block_order.shape, block_order.dtype),
            vmem((cycle, latent, rows), bf16),
            vmem((cycle, rows, dim), bf16),
            vmem((heads, latent, rows), bf16),
            vmem((rows, idx_heads, dim), bf16),
            vmem((idx_heads * rows, dim), bf16),
            vmem((idx_heads, rows), bf16),
            vmem((heads, rows), f32),
            vmem((2 * rows, latent), bf16),
            vmem((dim, cycle * rows), bf16),
            vmem((cycle * rows, idx_heads * rows), bf16),
            vmem((2 * rows, rows), f32),
            vmem((shares, groups + 1, share, 2 * rows), f32),
            vmem((shares, groups + 1, share, 2 * rows), bf16),
            vmem((shares, groups + 1, share, 2 * rows), f32),
            vmem((shares, groups + 1, share, 2 * rows), bf16),
            vmem((shares, groups + 1, share, 2 * rows), bf16),
            vmem((groups, 2, rows, dim), bf16),
            vmem((groups, 2, rows, dim), bf16),
            vmem((2, rows, dim), f32),
            vmem((rows, dim), f32),
            vmem((rows, dim), bf16),
            vmem((shares, rows // shares, dim), bf16),
            dma((7,)),
            dma((2, groups)), dma((2, groups)), dma((2, groups)), dma((2, groups)),
            dma((2, groups + 1, shares)), dma((2, groups + 1, shares)),
            dma((groups + 1, shares)), dma((groups + 1, shares)),
            dma((groups, 2)), dma((groups, 2)),
            dma((shares,)), dma((shares,)),
        ],
        compiler_params=pltpu.CompilerParams(collective_id=0, has_side_effects=True),
        name="indexer",
    )(
        block_order, key_latent.T, indexer_key, indexer_query, indexer_weight.T,
        query_latent.transpose(1, 2, 0), normalizer.T,
    )
    results = [pltpu.with_memory_space_constraint(x, pltpu.VMEM) for x in results]
    return pl.pallas_call(
        store,
        out_shape=(
            jax.ShapeDtypeStruct((rows, idx_heads, dim), f32),
            jax.ShapeDtypeStruct((rows // shares, dim), f32),
        ),
        in_specs=[pl.BlockSpec(memory_space=pltpu.VMEM)] * 2,
        out_specs=(pl.BlockSpec(memory_space=pl.ANY),) * 2,
        scratch_shapes=[dma((2,))],
        name="store",
    )(*results)


def solution(mesh):
    return jax.shard_map(
        per_device,
        mesh=mesh,
        in_specs=(
            P(),
            P("ctx", "head", None),
            P("ctx", None),
            P("ctx", "head"),
            P("ctx", "head", None),
            P("ctx", None),
            P("ctx", "head"),
        ),
        out_specs=(P("ctx", "head", None), P(("ctx", "head"), None)),
        check_vma=False,
    )
```

```python
import functools
import math

import jax
import jax.numpy as jnp
from jax import lax
from jax.experimental import pallas as pl
from jax.experimental.pallas import tpu as pltpu
from jax.sharding import PartitionSpec as P

MESH = pl.DeviceIdType.MESH
mla_scale = 192.0 ** (-0.5)
loss_scale = 64.0
log2e = math.log2(math.e)
NT_DIMS = (((1,), (1,)), ((), ()))


def remote(src, dst, send, recv, device):
    return pltpu.make_async_remote_copy(
        src_ref=src, dst_ref=dst, send_sem=send, recv_sem=recv, device_id=device, device_id_type=MESH
    )


def partner(group, step, groups):
    bit = 1
    while bit < groups:
        if step & bit:
            group = group + bit * (1 - 2 * lax.rem(group // bit, 2))
        bit *= 2
    return group


def kernel(
    groups, shares, order_far, lat, idx, iq, iw_far, q_far, norm_far, qg, kg_out,
    order,
    all_lat, all_idx, q, iq_near, iqf, iw, norm, keys, keys_t, coefs, rate,
    lsend, tsend, lrecv, trecv, gall, ksend, krecv, kown, kz, kzs, kzr,
    local, ds, dr, fs, fr, xs, xr, gs, gr, ks, kr, zs, zr,
):
    ctx, head = lax.axis_index("ctx"), lax.axis_index("head")
    group, core = ctx // 2, lax.rem(ctx, 2)
    sibling = group * 2 + 1 - core
    blocks = order.shape[0]
    rows, dim = idx.shape
    half = rows // 2
    share = half // shares
    heads, idx_heads = q.shape[0], iw.shape[0]
    bundle = 8
    idx_scale = (idx_heads * shares * dim) ** (-0.5)

    own = [
        pltpu.make_async_copy(iq, iq_near, local.at[0]),
        pltpu.make_async_copy(iw_far, iw, local.at[1]),
        pltpu.make_async_copy(idx, all_idx.at[ctx], local.at[2]),
        pltpu.make_async_copy(lat, all_lat.at[ctx], local.at[3]),
        pltpu.make_async_copy(norm_far, norm, local.at[4]),
        pltpu.make_async_copy(q_far, q, local.at[5]),
        pltpu.make_async_copy(order_far, order, local.at[6]),
    ]
    barrier = pltpu.get_barrier_semaphore()
    for step in range(1, groups):
        peer = partner(group, step, groups) * 2
        for j in range(2):
            pl.semaphore_signal(barrier, 1, device_id={"ctx": peer + j}, device_id_type=MESH)
    pl.semaphore_signal(barrier, 1, device_id={"ctx": sibling}, device_id_type=MESH)
    for step in range(1, shares):
        peer = partner(head, step, shares)
        pl.semaphore_signal(barrier, 1, device_id={"head": peer}, device_id_type=MESH)
    for copy in own:
        copy.start()
    pl.semaphore_wait(barrier, 2 * (groups - 1) + 1 + shares - 1)

    sent = []

    def go(copy):
        copy.start()
        sent.append(copy)

    def spread(k, step):
        src, dst = ((idx, all_idx), (lat, all_lat))[k]
        if step:
            peer = partner(group, step, groups) * 2 + core
            go(remote(src, dst.at[ctx], ds.at[k, step], dr.at[k, step], {"ctx": peer}))
        else:
            go(remote(src, dst.at[ctx], fs.at[k, 0], fr.at[k, 0], {"ctx": sibling}))

    near = min(3, groups)
    for k in range(2):
        spread(k, 0)
    for k in range(2):
        for step in range(1, near):
            spread(k, step)
    for step in range(near, groups):
        for k in range(2):
            spread(k, step)

    def relay(k, step):
        source = partner(group, step, groups) * 2 + core
        slot = (all_idx, all_lat)[k].at[source]
        remote(slot, slot, ds.at[k, step], dr.at[k, step], {"ctx": sibling}).wait_recv()
        go(remote(slot, slot, fs.at[k, step], fr.at[k, step], {"ctx": sibling}))

    def arrive(k, step):
        slot = (all_idx, all_lat)[k].at[partner(group, step, groups) * 2 + 1 - core]
        remote(slot, slot, fs.at[k, step], fr.at[k, step], {"ctx": sibling}).wait_recv()

    def swapped(c):
        return order[2 * c] >= blocks // 2

    def lowest(c):
        return jnp.minimum(order[2 * c], order[2 * c + 1])

    own[6].wait()
    mine_swapped, mine = swapped(ctx), lowest(ctx)
    lane = lax.broadcasted_iota(jnp.int32, (half, rows), 1)

    def turn(x):
        return pltpu.roll(x, half, 1)

    def pack(total, source):
        total = total.T
        first, second = total[:half], total[half:]
        hi = jnp.where(mine_swapped, first, second)
        lo = jnp.where(mine_swapped, second, first)
        packed, low = [], []
        for j in range(2):
            c = 2 * source + j
            flip, early = swapped(c), lowest(c) < mine
            h, l = hi[:, j * rows : (j + 1) * rows], lo[:, j * rows : (j + 1) * rows]
            a = jnp.where(flip, turn(h), h)
            b = jnp.where(flip, l, turn(l))
            packed.append(jnp.where(early & (lane >= half), b, a))
            low.append(b)
        return jnp.concatenate(packed, axis=1), jnp.where(core == 0, low[0], low[1])

    def unpack(slot, source):
        piece = jnp.concatenate([gall[z, slot] for z in range(shares)], axis=0)
        piece = piece.astype(jnp.float32)
        his, los = [], []
        for j in range(2):
            c = 2 * source + j
            flip, early = swapped(c), lowest(c) < mine
            x = piece[:, j * rows : (j + 1) * rows]
            low_lanes = early & (lane >= half)
            h = jnp.where(low_lanes, 0.0, x)
            l = jnp.where(low_lanes, x, 0.0)
            if slot == 0:
                extra = jnp.concatenate(
                    [gall[z, groups, :, :rows] for z in range(shares)], axis=0
                ).astype(jnp.float32)
                l = jnp.where(core == j, extra, l)
            his.append(jnp.where(flip, turn(h), h))
            los.append(jnp.where(flip, l, turn(l)))
        hi, lo = jnp.concatenate(his, axis=1), jnp.concatenate(los, axis=1)
        first = jnp.where(mine_swapped, hi, lo)
        second = jnp.where(mine_swapped, lo, hi)
        return jnp.concatenate((first, second), axis=0).T

    def exchange(k, slot, width):
        send, recv = ((lsend, lrecv), (tsend, trecv))[k]
        for step in range(shares - 1, 0, -1):
            peer = partner(head, step, shares)
            go(
                remote(
                    send.at[peer, slot, :, pl.ds(0, width)],
                    recv.at[step, slot, :, pl.ds(0, width)],
                    xs.at[k, slot, step], xr.at[k, slot, step], {"head": peer},
                )
            )

    def deal(k, slot, packed):
        send = (lsend, tsend)[k]
        for z in range(shares):
            send[z, slot, :, : packed.shape[1]] = packed[z * share : (z + 1) * share].astype(
                send.dtype
            )
        exchange(k, slot, packed.shape[1])

    def logits(step):
        source = partner(group, step, groups)
        chip = jnp.concatenate((all_idx[2 * source], all_idx[2 * source + 1]), axis=0)
        keys_t[:, step * 2 * rows : (step + 1) * 2 * rows] = chip.T
        total = jnp.zeros((2 * rows, rows), jnp.float32)
        for p in range(idx_heads // 2):
            cols = slice(2 * p * rows, 2 * (p + 1) * rows)
            dots = lax.dot_general(
                chip, iqf[cols, :], NT_DIMS, preferred_element_type=jnp.float32
            )
            coefs[step * 2 * rows : (step + 1) * 2 * rows, cols] = jnp.where(
                dots > 0, 1.0, 0.0
            ).astype(jnp.bfloat16)
            dots = jnp.maximum(dots, 0.0)
            total = total + dots[:, :rows] * weights[2 * p : 2 * p + 1]
            total = total + dots[:, rows:] * weights[2 * p + 1 : 2 * p + 2]
        packed, low = pack(total, source)
        deal(0, step, packed)
        if step == 0:
            deal(0, groups, low)

    def attend(lhs):
        total = jnp.zeros((lhs.shape[0], rows), jnp.float32)
        for h in range(0, heads, 2):
            pair = jnp.concatenate((q[h], q[h + 1]), axis=1)
            scores = jnp.dot(lhs[...], pair, preferred_element_type=jnp.float32) * (
                mla_scale * log2e
            )
            shift = norm[h : h + 2, :] * log2e
            total = total + jnp.exp2(scores[:, :rows] - shift[:1])
            total = total + jnp.exp2(scores[:, rows:] - shift[1:])
        return total

    def score(step, split):
        source = partner(group, step, groups)
        if split:
            parts = []
            for k, device in enumerate((2 * source + core, 2 * source + 1 - core)):
                if k:
                    arrive(1, step)
                half_keys = keys.at[pl.ds(k * rows, rows)]
                half_keys[...] = all_lat[device].T
                parts.append(attend(half_keys))
            total = jnp.concatenate(
                (jnp.where(core == 0, *parts), jnp.where(core == 0, *parts[::-1])), axis=0
            )
        else:
            arrive(1, step)
            keys[...] = jnp.concatenate((all_lat[2 * source], all_lat[2 * source + 1]), axis=1).T
            total = attend(keys)
        packed, low = pack(total, source)
        deal(1, step, packed)
        if step == 0:
            deal(1, groups, low)

    own[0].wait()
    iqf[...] = jnp.swapaxes(iq_near[...], 0, 1).reshape(idx_heads * rows, dim)
    own[1].wait()
    weights = iw[...].astype(jnp.float32) * idx_scale
    own[2].wait()
    arrive(0, 0)
    logits(0)
    for step in range(1, near):
        relay(0, step)
    for copy in own[3:6]:
        copy.wait()
    score(0, False)
    for step in range(1, near):
        arrive(0, step)
        logits(step)
    for step in range(1, near):
        relay(1, step)
    for step in range(1, groups):
        if near <= step + 1 < groups:
            relay(0, step + 1)
        if step >= near:
            arrive(0, step)
            logits(step)
            relay(1, step)
        score(step, step != near - 1)

    shape = (share, 2 * rows)
    token = head * share + lax.broadcasted_iota(jnp.int32, shape, 0)
    column = lax.broadcasted_iota(jnp.int32, shape, 1)
    inner = lax.rem(column, rows)
    later = inner >= half

    def columns(slot):
        if slot == groups:
            seen = later & (inner - half <= token)
            return later[:, :rows], seen[:, :rows], rows
        source = partner(group, slot, groups)
        early = [(lowest(2 * source + j) < mine).astype(jnp.int32) for j in range(2)]
        low = later & (jnp.where(column < rows, early[0], early[1]) > 0)
        seen = None
        if slot == 0:
            mixed = (column >= core * rows) & (column < (core + 1) * rows) & later
            seen = jnp.logical_not(mixed) | (inner - half <= token)
        return low, seen, 2 * rows

    slots = [*range(groups - 1, near - 1, -1), *range(1, near), 0, groups]
    table = {slot: columns(slot) for slot in slots}

    def gather_sum(k, slot):
        send, recv = ((lsend, lrecv), (tsend, trecv))[k]
        width = table[slot][2]
        value = send[head, slot, :, :width].astype(jnp.float32)
        for step in range(1, shares):
            piece = recv.at[step, slot, :, pl.ds(0, width)]
            remote(piece, piece, xs.at[k, slot, step], xr.at[k, slot, step], {"head": head}).wait_recv()
            value = value + recv[step, slot, :, :width].astype(jnp.float32)
        return value

    inf = jnp.float32(jnp.inf)

    def split(values, reduce, fill):
        his, los = [], []
        for slot, value in values.items():
            low, seen, _ = table[slot]
            h = low if seen is None else low | jnp.logical_not(seen)
            l = jnp.logical_not(low) if seen is None else jnp.logical_not(low & seen)
            his.append(reduce(jnp.where(h, fill, value), axis=1, keepdims=True))
            los.append(reduce(jnp.where(l, fill, value), axis=1, keepdims=True))
        return his, los

    scored = {slot: gather_sum(0, slot) for slot in slots}
    his, los = split(scored, jnp.max, -inf)
    hi_top, lo_top = functools.reduce(jnp.maximum, his), functools.reduce(jnp.maximum, los)
    scored = {
        slot: jnp.exp(value - jnp.where(table[slot][0], lo_top, hi_top))
        for slot, value in scored.items()
    }
    his, los = split(scored, jnp.sum, 0.0)
    hi_norm, lo_norm = loss_scale / sum(his), loss_scale / sum(los)
    target = {slot: gather_sum(1, slot) for slot in slots}
    his, los = split(target, jnp.sum, 0.0)
    hi_total, lo_total = loss_scale / sum(his), loss_scale / sum(los)
    for slot in slots:
        low, seen, width = table[slot]
        value = scored[slot] * jnp.where(low, lo_norm, hi_norm)
        value = value - target[slot] * jnp.where(low, lo_total, hi_total)
        if seen is not None:
            value = jnp.where(seen, value, 0.0)
        gall[head, slot, :, :width] = value.astype(jnp.bfloat16)
        for step in range(shares - 1, 0, -1):
            peer = partner(head, step, shares)
            piece = gall.at[head, slot, :, pl.ds(0, width)]
            go(remote(piece, piece, gs.at[slot, step], gr.at[slot, step], {"head": peer}))

    def granted(slot):
        for step in range(1, shares):
            source = partner(head, step, shares)
            piece = gall.at[source, slot, :, pl.ds(0, table[slot][2])]
            remote(piece, piece, gs.at[slot, step], gr.at[slot, step], {"head": source}).wait_recv()

    for slot in [*range(groups - 1, near - 1, -1), *range(1, near), 0]:
        granted(slot)
        if slot == 0:
            granted(groups)
        source = partner(group, slot, groups)
        rate[...] = unpack(slot, source)
        span = slice(slot * 2 * rows, (slot + 1) * 2 * rows)
        total = jnp.zeros((2 * rows, dim), jnp.float32)
        for p in range(idx_heads // 2):
            cols = slice(2 * p * rows, 2 * (p + 1) * rows)
            value = jnp.concatenate(
                [rate[...] * weights[h : h + 1] for h in (2 * p, 2 * p + 1)], axis=1
            ).astype(jnp.bfloat16) * coefs[span, cols]
            coefs[span, cols] = value
            total = total + jnp.dot(value, iqf[cols, :], preferred_element_type=jnp.float32)
        if slot == 0:
            kown[...] = total.reshape(2, rows, dim)
        ksend[slot] = total.astype(jnp.bfloat16).reshape(2, rows, dim)
        if slot == 0:
            go(
                remote(
                    ksend.at[0, 1 - core], krecv.at[0, core], ks.at[0, 0], kr.at[0, core],
                    {"ctx": sibling},
                )
            )
        else:
            for j in range(2):
                go(
                    remote(
                        ksend.at[slot, j], krecv.at[slot, core], ks.at[slot, j], kr.at[slot, core],
                        {"ctx": source * 2 + j},
                    )
                )

    def query(p):
        cols = slice(2 * p * rows, 2 * (p + 1) * rows)
        value = jnp.dot(keys_t[...], coefs[:, cols], preferred_element_type=jnp.float32).T
        qg[:, 2 * p, :] = value[:rows]
        qg[:, 2 * p + 1, :] = value[rows:]

    pairs = idx_heads // 2
    for p in range(pairs // 2):
        query(p)
    value = kown[core]
    for slot in [*range(groups - 1, near - 1, -1), *range(1, near), 0]:
        for k in range(2) if slot else (1 - core,):
            piece = krecv.at[slot, k]
            remote(piece, piece, ks.at[slot, 0], kr.at[slot, k], {"ctx": sibling}).wait_recv()
            value = value + krecv[slot, k].astype(jnp.float32)
    kz[...] = value
    kzs[...] = value.astype(jnp.bfloat16)
    part = rows // shares
    for step in range(shares - 1, 0, -1):
        peer = partner(head, step, shares)
        take = pl.ds(pl.multiple_of(peer * part, part), part)
        go(remote(kzs.at[take], kzr.at[step], zs.at[step], zr.at[step], {"head": peer}))
    for p in range(pairs // 2, pairs):
        query(p)
    value = kz[pl.ds(pl.multiple_of(head * part, part), part), :]
    for step in range(1, shares):
        remote(kzr.at[step], kzr.at[step], zs.at[step], zr.at[step], {"head": head}).wait_recv()
        value = value + kzr[step].astype(jnp.float32)
    kg_out[...] = value
    for copy in sent:
        copy.wait_send()


def store(qg, kg, qg_out, kg_out, sems):
    copies = [
        pltpu.make_async_copy(qg, qg_out, sems.at[0]), pltpu.make_async_copy(kg, kg_out, sems.at[1])
    ]
    for copy in copies:
        copy.start()
    for copy in copies:
        copy.wait()


def per_device(
    block_order, query_latent, key_latent, normalizer, indexer_query, indexer_key, indexer_weight
):
    cycle, shares = lax.axis_size("ctx"), lax.axis_size("head")
    groups = cycle // 2
    rows, dim = indexer_key.shape
    heads, latent = query_latent.shape[1:]
    idx_heads = indexer_query.shape[1]
    share = rows // 2 // shares
    bf16, f32 = jnp.bfloat16, jnp.float32
    dma, vmem = pltpu.SemaphoreType.DMA, pltpu.VMEM
    results = pl.pallas_call(
        functools.partial(kernel, groups, shares),
        out_shape=(
            vmem((rows, idx_heads, dim), f32),
            vmem((rows // shares, dim), f32),
        ),
        in_specs=[pl.BlockSpec(memory_space=pl.ANY)] * 7,
        out_specs=(pl.BlockSpec(memory_space=pltpu.VMEM),) * 2,
        scratch_shapes=[
            pltpu.SMEM(block_order.shape, block_order.dtype),
            vmem((cycle, latent, rows), bf16),
            vmem((cycle, rows, dim), bf16),
            vmem((heads, latent, rows), bf16),
            vmem((rows, idx_heads, dim), bf16),
            vmem((idx_heads * rows, dim), bf16),
            vmem((idx_heads, rows), bf16),
            vmem((heads, rows), f32),
            vmem((2 * rows, latent), bf16),
            vmem((dim, cycle * rows), bf16),
            vmem((cycle * rows, idx_heads * rows), bf16),
            vmem((2 * rows, rows), f32),
            vmem((shares, groups + 1, share, 2 * rows), f32),
            vmem((shares, groups + 1, share, 2 * rows), bf16),
            vmem((shares, groups + 1, share, 2 * rows), f32),
            vmem((shares, groups + 1, share, 2 * rows), bf16),
            vmem((shares, groups + 1, share, 2 * rows), bf16),
            vmem((groups, 2, rows, dim), bf16),
            vmem((groups, 2, rows, dim), bf16),
            vmem((2, rows, dim), f32),
            vmem((rows, dim), f32),
            vmem((rows, dim), bf16),
            vmem((shares, rows // shares, dim), bf16),
            dma((7,)),
            dma((2, groups)), dma((2, groups)), dma((2, groups)), dma((2, groups)),
            dma((2, groups + 1, shares)), dma((2, groups + 1, shares)),
            dma((groups + 1, shares)), dma((groups + 1, shares)),
            dma((groups, 2)), dma((groups, 2)),
            dma((shares,)), dma((shares,)),
        ],
        compiler_params=pltpu.CompilerParams(collective_id=0, has_side_effects=True),
        name="indexer",
    )(
        block_order, key_latent.T, indexer_key, indexer_query, indexer_weight.T,
        query_latent.transpose(1, 2, 0), normalizer.T,
    )
    results = [pltpu.with_memory_space_constraint(x, pltpu.VMEM) for x in results]
    return pl.pallas_call(
        store,
        out_shape=(
            jax.ShapeDtypeStruct((rows, idx_heads, dim), f32),
            jax.ShapeDtypeStruct((rows // shares, dim), f32),
        ),
        in_specs=[pl.BlockSpec(memory_space=pltpu.VMEM)] * 2,
        out_specs=(pl.BlockSpec(memory_space=pl.ANY),) * 2,
        scratch_shapes=[dma((2,))],
        name="store",
    )(*results)


def solution(mesh):
    return jax.shard_map(
        per_device,
        mesh=mesh,
        in_specs=(
            P(),
            P("ctx", "head", None),
            P("ctx", None),
            P("ctx", "head"),
            P("ctx", "head", None),
            P("ctx", None),
            P("ctx", "head"),
        ),
        out_specs=(P("ctx", "head", None), P(("ctx", "head"), None)),
        check_vma=False,
    )
```
